32 devices in a mesh: dp: 16 (over z, y, core), tensor: 2 (over x).
Axes of the slice: x: 2, y: 2, z: 4, core: 2. Of those that a mesh axis runs over, the one named last changes fastest.
Arguments:
- tokens: bfloat16 [16384, 4096], P(('dp', 'tensor')), may hold values from -6 to 6
- out_grad: bfloat16 [16384, 2048], P('dp', 'tensor'), may hold values from -6 to 6
- weights: bfloat16 [4096, 2, 2048], P(None, None, 'tensor'), may hold values from -0.09375 to 0.09375
- master: float32 [4096, 2, 2048], P('dp', None, 'tensor'), may hold values from -0.09375 to 0.09375
- first_moment: float32 [4096, 2, 2048], P('dp', None, 'tensor'), may hold values from -4 to 4
- second_moment: float32 [4096, 2, 2048], P('dp', None, 'tensor'), may hold values from 0.05 to 5
Outputs:
- input_grad: bfloat16 [16384, 4096], P(('dp', 'tensor'))
- new_weights: bfloat16 [4096, 2, 2048], P(None, None, 'tensor')
- new_master: float32 [4096, 2, 2048], P('dp', None, 'tensor')
- new_first: float32 [4096, 2, 2048], P('dp', None, 'tensor')
- new_second: float32 [4096, 2, 2048], P('dp', None, 'tensor')
The draws below stay inside these ranges and needn't reach their ends.
All inputs are finite; a program needn't handle non-finite values.
Results may differ from the reference program's by a relative error of at most 0.012.
Values may be sent and summed in bfloat16 or wider, within the bound.
A program may use at most 192 MiB of HBM per device.

```python
import math
import jax
import jax.numpy as jnp
from jax import lax

D = 4096
HID = 2048
SEQ = 512
BATCH = 2
TOKENS_ALL = 16384
N_DP = 16
N_TENSOR = 2


def raised(values, stream_key, source, target, shards_of, factor):
    owner, partner = [(jnp.arange(values.shape[axis_at]) // (values.shape[axis_at] // shards_of)).reshape([-1 if axis == axis_at else 1 for axis in range(values.ndim)]) for axis_at in (source, target)]
    chosen = jax.random.permutation(stream_key, shards_of)[partner]
    strong = (owner == chosen) | (owner == (partner + shards_of // 2) % shards_of)
    return jnp.where(strong, factor * values, values)


def block_levels(key, shape, cuts, least, largest):
    def one(position, blocks):
        steps = jax.random.uniform(jax.random.fold_in(jax.random.fold_in(key, 6), position), (blocks,), jnp.float32, least / len(cuts), largest / len(cuts))
        return jnp.repeat(jnp.exp(steps), shape[position] // blocks).reshape((-1,) + (1,) * (len(shape) - position - 1))

    gain = one(*cuts[0])
    for cut in cuts[1:]:
        gain = gain * one(*cut)
    return gain


def gaussian(stream_key, extent, scale, most, pieces=(), held_as=jnp.bfloat16):
    drawn = jax.random.normal(stream_key, extent, jnp.float32) * scale
    if len(pieces) > 0:
        drawn = block_levels(stream_key, extent, pieces, -0.22, 0.18) * drawn
    return jnp.clip(drawn, min=-most, max=most).astype(held_as)


def heavy_noise(rng, dims, scale, reach, pieces, heavy, held_as=jnp.bfloat16):
    drawn = scale * jax.random.normal(rng, dims, jnp.float32)
    if pieces:
        drawn = drawn * block_levels(rng, dims, pieces, -0.22, 0.18)
    return jnp.clip(raised(drawn, jax.random.fold_in(rng, 3), *heavy), -reach, reach).astype(held_as)


def setup_inputs(seed: int = 0) -> dict:
    streams_of = jax.random.split(jax.random.key(seed), 7)
    tokens = heavy_noise(streams_of[0], (TOKENS_ALL, D), 1.0, 6.0, ((0, 32),), (0, 1, 32, 2.75))
    out_grad = gaussian(streams_of[1], (TOKENS_ALL, HID), 1.0, 6.0, ((0, 16), (1, 2)))
    weights = gaussian(streams_of[2], (D, 2, HID), D ** -0.5, 0.09375, ((2, 2),))
    master = gaussian(streams_of[3], (D, 2, HID), D ** -0.5, 0.09375, ((0, 16), (2, 2)), jnp.float32)
    first_moment = gaussian(streams_of[4], (D, 2, HID), 0.5, 4.0, ((0, 16), (2, 2)), jnp.float32)
    second_moment = jnp.clip(jnp.exp(math.log(5.0) - 4.6051702 * jax.random.uniform(streams_of[5], (D, 2, HID), jnp.float32) ** block_levels(streams_of[5], (D, 2, HID), ((0, 16), (2, 2)), -0.2, 0.2)), 0.05, 5.0)
    return {"tokens": tokens, "out_grad": out_grad, "weights": weights, "master": master, "first_moment": first_moment, "second_moment": second_moment}


def linear_step(earlier, latter):
    return (earlier[0] * latter[0], latter[0] * earlier[1] + latter[1])

def local_backward(projected, out_grad):
    token_count = projected.shape[0]
    hidden_width = projected.shape[1] // 2
    shaped = (token_count // SEQ, SEQ, hidden_width)
    gate_value = jax.nn.sigmoid(projected[:, :hidden_width]).reshape(shaped)
    candidate = projected[:, hidden_width:].reshape(shaped)
    upstream = out_grad.astype(jnp.float32).reshape(shaped)
    retain = 1.0 - gate_value
    _, hidden_state = lax.associative_scan(linear_step, (retain, gate_value * candidate), axis=1)
    zeros_row = jnp.zeros_like(hidden_state[:, :1])
    previous = jnp.concatenate([zeros_row, hidden_state[:, :-1]], axis=1)
    retain_next = jnp.concatenate([retain[:, 1:], zeros_row], axis=1)
    _, flipped = lax.associative_scan(linear_step, (jnp.flip(retain_next, axis=1), jnp.flip(upstream, axis=1)), axis=1)
    adjoint = jnp.flip(flipped, axis=1)
    gate_grad = adjoint * (candidate - previous) * gate_value * retain
    candidate_grad = adjoint * gate_value
    joined = jnp.concatenate([gate_grad, candidate_grad], axis=2)
    return joined.reshape(token_count, 2 * hidden_width).astype(jnp.bfloat16)

def reference(tokens, out_grad, weights, master, first_moment, second_moment):
    token_count = BATCH * SEQ
    half_width = HID // N_TENSOR
    flat_weights = weights.reshape(D, 2 * HID)
    weight_parts = weights.reshape(D, 2, N_TENSOR, half_width)
    token_sets = tokens.reshape(N_DP, token_count, D)
    grad_sets = out_grad.reshape(N_DP, token_count, HID)

    def replica(running, element):
        inputs, upstream = element
        projected = jnp.dot(inputs, flat_weights, preferred_element_type=jnp.float32)
        pre_grad = local_backward(projected, upstream)
        grad_parts = pre_grad.reshape(token_count, 2, N_TENSOR, half_width)

        def shard_term(summed, shard_index):
            selected = lax.dynamic_index_in_dim(grad_parts, shard_index, 2, keepdims=False).reshape(token_count, 2 * half_width)
            columns = lax.dynamic_index_in_dim(weight_parts, shard_index, 2, keepdims=False).reshape(D, 2 * half_width)
            partial_value = lax.dot_general(selected, columns, (((1,), (1,)), ((), ())), preferred_element_type=jnp.float32)
            rounded = lax.optimization_barrier(partial_value.astype(jnp.bfloat16))
            return (summed + rounded.astype(jnp.float32), None)
        summed, _ = lax.scan(shard_term, jnp.zeros((token_count, D), jnp.float32), jnp.arange(N_TENSOR, dtype=jnp.int32))
        replica_grad = lax.dot_general(inputs, pre_grad, (((0,), (0,)), ((), ())), preferred_element_type=jnp.float32)
        return (running + replica_grad, summed.astype(jnp.bfloat16))
    gradient_sum, input_sets = lax.scan(replica, jnp.zeros((D, 2 * HID), jnp.float32), (token_sets, grad_sets))
    input_grad = input_sets.reshape(N_DP * token_count, D)
    gradient = gradient_sum.reshape(D, 2, HID) * (token_count * N_DP) ** (-0.5)
    new_first = 0.9 * first_moment + 0.1 * gradient
    new_second = 0.95 * second_moment + 0.05 * gradient * gradient
    update = new_first / (1.0 - 0.9 ** 10) / (jnp.sqrt(new_second / (1.0 - 0.95 ** 10)) + 1e-08)
    new_master = master - 0.001 * (update + 0.1 * master)
    return (input_grad, new_master.astype(jnp.bfloat16), new_master, new_first, new_second)
```

```python
import jax
import jax.numpy as jnp
from jax import lax
from jax.experimental import pallas as pl
from jax.experimental.pallas import tpu as pltpu
from jax.sharding import PartitionSpec as P

SEQ = 512
ROWS = 8
STEP = 16
BF16 = jnp.bfloat16
F32 = jnp.float32


def scan_kernel(gate_ref, cand_ref, up_ref, out_ref, z_ref, m_ref):
    seq, width = gate_ref.shape
    half_width = out_ref.shape[1] // 2
    column = pl.multiple_of(pl.program_id(1) * width, width)
    row = lax.broadcasted_iota(jnp.int32, (ROWS, width), 0)

    def down(values, count, fill):
        return jnp.where(row >= count, pltpu.roll(values, count, 0), fill)

    def up(values, count, fill):
        return jnp.where(row < ROWS - count, pltpu.roll(values, ROWS - count, 0), fill)

    def spread(values, index):
        return jnp.broadcast_to(values[index : index + 1], (ROWS, width))

    def solve(shift, factor, term, carry):
        for count in (1, 2, 4):
            term = term + factor * shift(term, count, 0.0)
            factor = factor * shift(factor, count, 1.0)
        return term + factor * carry

    def forward(index, carry):
        start = pl.multiple_of(index * STEP, STEP)
        for part in range(STEP // ROWS):
            rows = pl.ds(start + part * ROWS, ROWS)
            z = jax.nn.sigmoid(gate_ref[rows, :])
            c = cand_ref[rows, :]
            r = 1.0 - z
            h = solve(down, r, z * c, carry)
            previous = down(h, 1, carry)
            z_ref[rows, :] = z
            m_ref[rows, :] = (c - previous) * z * r
            carry = spread(h, ROWS - 1)
        return carry

    def backward(index, carry):
        start = pl.multiple_of(seq - STEP - index * STEP, STEP)
        upstream = up_ref[pl.ds(start, STEP), :].astype(F32)
        gates, cands = [], []
        for part in reversed(range(STEP // ROWS)):
            rows = pl.ds(start + part * ROWS, ROWS)
            z = z_ref[rows, :]
            r = 1.0 - z
            u = upstream[part * ROWS : (part + 1) * ROWS]
            q = solve(up, r, r * u, carry)
            g = u + up(q, 1, carry)
            gates.insert(0, g * m_ref[rows, :])
            cands.insert(0, g * z)
            carry = spread(q, 0)
        out_ref[pl.ds(start, STEP), pl.ds(column, width)] = jnp.concatenate(gates, 0).astype(BF16)
        out_ref[pl.ds(start, STEP), pl.ds(half_width + column, width)] = jnp.concatenate(
            cands, 0
        ).astype(BF16)
        return carry

    zero = jnp.zeros((ROWS, width), F32)
    lax.fori_loop(0, seq // STEP, forward, zero, unroll=2)
    lax.fori_loop(0, seq // STEP, backward, zero, unroll=2)


def local_backward(projected, out_grad):
    tokens, both = projected.shape
    half_width = both // 2
    width = min(512, half_width)
    blocks = half_width // width
    return pl.pallas_call(
        scan_kernel,
        grid=(tokens // SEQ, blocks),
        in_specs=[
            pl.BlockSpec((SEQ, width), lambda b, j: (b, j)),
            pl.BlockSpec((SEQ, width), lambda b, j: (b, j + blocks)),
            pl.BlockSpec((SEQ, width), lambda b, j: (b, j)),
        ],
        out_specs=pl.BlockSpec((SEQ, both), lambda b, j: (b, 0)),
        out_shape=jax.ShapeDtypeStruct((tokens, both), BF16),
        scratch_shapes=[pltpu.VMEM((SEQ, width), F32), pltpu.VMEM((SEQ, width), F32)],
        cost_estimate=pl.CostEstimate(
            flops=tokens * half_width * 80, bytes_accessed=tokens * half_width * 14, transcendentals=0
        ),
    )(projected, projected, out_grad)


def adamw_update(gradient, master, first_moment, second_moment):
    new_first = 0.9 * first_moment + 0.1 * gradient
    new_second = 0.95 * second_moment + 0.05 * gradient * gradient
    update = new_first / (1.0 - 0.9**10) / (jnp.sqrt(new_second / (1.0 - 0.95**10)) + 1e-08)
    new_master = master - 0.001 * (update + 0.1 * master)
    return (new_master, new_first, new_second)


def product(a, b, contract):
    return lax.dot_general(a, b, ((contract[:1], contract[1:]), ((), ())), preferred_element_type=F32)


def body(tokens, out_grad, weights, master, first_moment, second_moment):
    model_width, _, half_width = weights.shape
    both = 2 * half_width
    flat_weights = weights.reshape(model_width, both)
    local_tokens = tokens.shape[0]
    replicas = lax.axis_size("dp")
    shards = lax.axis_size("tensor")
    shard = lax.axis_index("tensor")
    core = lax.axis_index("dp") % 2
    chips = replicas // 2
    share = model_width // replicas
    loss_scale = (local_tokens * shards * replicas) ** (-0.5)
    swap = [(i, i ^ 1) for i in range(replicas)]
    groups = [[i for i in range(replicas) if i % 2 == c] for c in range(2)]

    def columns_of(block, c):
        cut = block.reshape(block.shape[0], chips, 2, share)
        return lax.dynamic_index_in_dim(cut, c, 2, keepdims=False)

    whole = local_tokens % SEQ == 0
    if whole:
        blocks = [tokens]
        for k in range(1, shards):
            blocks.append(lax.ppermute(tokens, "tensor", [(i, (i + k) % shards) for i in range(shards)]))
        ups = [
            lax.dynamic_slice_in_dim(out_grad, ((shard - k) % shards) * local_tokens, local_tokens, 0)
            for k in range(shards)
        ]
    else:
        blocks = [lax.all_gather(tokens, "tensor", axis=0, tiled=True)]
        ups = [out_grad]

    mine_x, other_x, mine_p, other_p, terms = [], [], [], [], []
    for block, upstream in zip(blocks, ups):
        other_x.append(lax.ppermute(columns_of(block, 1 - core), "dp", swap))
        mine_x.append(columns_of(block, core))
        projected = jnp.dot(block, flat_weights, preferred_element_type=F32)
        pre_grad = local_backward(projected, upstream)
        mine_p.append(pre_grad)
        other_p.append(lax.ppermute(pre_grad, "dp", swap))
        terms.append(lambda p=pre_grad: product(p, flat_weights, (1, 1)).astype(BF16))

    parts = 1
    rows = share
    left = [jnp.concatenate([a, b], 0) for a, b in zip(mine_x, other_x)]
    right = [jnp.concatenate([a, b], 0) for a, b in zip(mine_p, other_p)]
    updated, gathered = [], []
    for part in range(parts):
        total = 0.0
        for a, b in zip(left, right):
            cut = a[:, :, part * rows : (part + 1) * rows].reshape(a.shape[0], chips * rows)
            total = total + product(cut, b, (0, 0))
        summed = lax.psum_scatter(
            total.astype(BF16), "dp", scatter_dimension=0, tiled=True, axis_index_groups=groups
        )
        gradient = (summed.astype(F32) * loss_scale).reshape(rows, 2, half_width)
        here = slice(part * rows, (part + 1) * rows)
        updated.append(adamw_update(gradient, master[here], first_moment[here], second_moment[here]))
        gathered.append(lax.all_gather(updated[-1][0].astype(BF16), "dp", axis=0, tiled=True))

    if whole:
        total = terms[0]().astype(F32)
        for k in range(1, shards):
            term = lax.ppermute(terms[k](), "tensor", [(i, (i - k) % shards) for i in range(shards)])
            total = total + term.astype(F32)
        input_grad = total.astype(BF16)
    else:
        input_grad = lax.psum_scatter(terms[0](), "tensor", scatter_dimension=0, tiled=True)

    news = [jnp.concatenate(values, 0) for values in zip(*updated)]
    return (input_grad, gathered[0], *news)


def solution(mesh):
    state = P("dp", None, "tensor")
    rows = P(("dp", "tensor"), None)
    held = P(None, None, "tensor")
    return jax.shard_map(
        body,
        mesh=mesh,
        in_specs=(rows, P("dp", "tensor"), held, state, state, state),
        out_specs=(rows, held, state, state, state),
        check_vma=False,
    )
```

```python
import functools

import jax
import jax.numpy as jnp
from jax import lax
from jax.experimental import pallas as pl
from jax.experimental.pallas import tpu as pltpu
from jax.sharding import PartitionSpec as P


SEQ = 512
ROWS = 8
STEP = 16

BF16 = jnp.bfloat16
F32 = jnp.float32


def scan_kernel(gate_ref, cand_ref, up_ref, out_ref, z_ref, m_ref):
    seq, width = gate_ref.shape
    half_width = out_ref.shape[1] // 2
    column = pl.multiple_of(pl.program_id(1) * width, width)
    row = lax.broadcasted_iota(jnp.int32, (ROWS, width), 0)

    def down(values, count, fill):
        return jnp.where(row >= count, pltpu.roll(values, count, 0), fill)

    def up(values, count, fill):
        return jnp.where(row < ROWS - count, pltpu.roll(values, ROWS - count, 0), fill)

    def spread(values, index):
        return jnp.broadcast_to(values[index : index + 1], (ROWS, width))

    def solve(shift, factor, term, carry):
        for count in (1, 2, 4):
            term = term + factor * shift(term, count, 0.0)
            factor = factor * shift(factor, count, 1.0)
        return term + factor * carry

    def forward(index, carry):
        start = pl.multiple_of(index * STEP, STEP)
        for part in range(STEP // ROWS):
            rows = pl.ds(start + part * ROWS, ROWS)
            z = jax.nn.sigmoid(gate_ref[rows, :])
            c = cand_ref[rows, :]
            r = 1.0 - z
            h = solve(down, r, z * c, carry)
            previous = down(h, 1, carry)
            z_ref[rows, :] = z
            m_ref[rows, :] = (c - previous) * z * r
            carry = spread(h, ROWS - 1)
        return carry

    def backward(index, carry):
        start = pl.multiple_of(seq - STEP - index * STEP, STEP)
        upstream = up_ref[pl.ds(start, STEP), :].astype(F32)
        gates, cands = [], []
        for part in reversed(range(STEP // ROWS)):
            rows = pl.ds(start + part * ROWS, ROWS)
            z = z_ref[rows, :]
            r = 1.0 - z
            u = upstream[part * ROWS : (part + 1) * ROWS]
            q = solve(up, r, r * u, carry)
            g = u + up(q, 1, carry)
            gates.insert(0, g * m_ref[rows, :])
            cands.insert(0, g * z)
            carry = spread(q, 0)
        out_ref[pl.ds(start, STEP), pl.ds(column, width)] = jnp.concatenate(gates, 0).astype(BF16)
        out_ref[pl.ds(start, STEP), pl.ds(half_width + column, width)] = jnp.concatenate(
            cands, 0
        ).astype(BF16)
        return carry

    zero = jnp.zeros((ROWS, width), F32)
    lax.fori_loop(0, seq // STEP, forward, zero, unroll=2)
    lax.fori_loop(0, seq // STEP, backward, zero, unroll=2)


def local_backward(projected, out_grad):
    tokens, both = projected.shape
    half_width = both // 2
    width = min(512, half_width)
    blocks = half_width // width
    return pl.pallas_call(
        scan_kernel,
        grid=(tokens // SEQ, blocks),
        in_specs=[
            pl.BlockSpec((SEQ, width), lambda b, j: (b, j)),
            pl.BlockSpec((SEQ, width), lambda b, j: (b, j + blocks)),
            pl.BlockSpec((SEQ, width), lambda b, j: (b, j)),
        ],
        out_specs=pl.BlockSpec((SEQ, both), lambda b, j: (b, 0)),
        out_shape=jax.ShapeDtypeStruct((tokens, both), BF16),
        scratch_shapes=[pltpu.VMEM((SEQ, width), F32), pltpu.VMEM((SEQ, width), F32)],
        cost_estimate=pl.CostEstimate(
            flops=tokens * half_width * 80, bytes_accessed=tokens * half_width * 14, transcendentals=0
        ),
    )(projected, projected, out_grad)


def adamw_update(gradient, master, first_moment, second_moment):
    new_first = 0.9 * first_moment + 0.1 * gradient
    new_second = 0.95 * second_moment + 0.05 * gradient * gradient
    update = new_first / (1.0 - 0.9**10) / (jnp.sqrt(new_second / (1.0 - 0.95**10)) + 1e-08)
    new_master = master - 0.001 * (update + 0.1 * master)
    return (new_master, new_first, new_second)


def product(a, b, contract):
    return lax.dot_general(a, b, ((contract[:1], contract[1:]), ((), ())), preferred_element_type=F32)


def columns_kernel(place_ref, source_ref, out_ref):
    out_ref[...] = source_ref[...]


def pick_columns(block, parity, share):
    tokens, width = block.shape
    return pl.pallas_call(
        columns_kernel,
        grid_spec=pltpu.PrefetchScalarGridSpec(
            num_scalar_prefetch=1,
            grid=(width // (2 * share),),
            in_specs=[pl.BlockSpec((tokens, share), lambda j, at: (0, 2 * j + at[0]))],
            out_specs=pl.BlockSpec((tokens, share), lambda j, at: (0, j)),
        ),
        out_shape=jax.ShapeDtypeStruct((tokens, width // 2), block.dtype),
        cost_estimate=pl.CostEstimate(
            flops=0, bytes_accessed=tokens * width * 2, transcendentals=0
        ),
    )(jnp.reshape(parity, (1,)), block)


def tile_kernel(count, place_ref, *refs):
    out_ref = refs[-1]
    total = jnp.zeros(out_ref.shape, F32)
    for a_ref, b_ref in zip(refs[:count], refs[count:-1]):
        total = total + product(a_ref[...], b_ref[...], (0, 0))
    out_ref[...] = total.astype(out_ref.dtype)


def tile_product(own, other, left, passed, right, share, dtype):
    both = right[0].shape[1]
    width = min(512, both)
    specs = [pl.BlockSpec((a.shape[0], share), lambda n, at: (0, at[0])) for a in left]
    specs += [pl.BlockSpec((a.shape[0], share), lambda n, at: (0, at[1])) for a in passed]
    specs += [pl.BlockSpec((b.shape[0], width), lambda n, at: (0, n)) for b in right]
    depth = sum(b.shape[0] for b in right)
    return pl.pallas_call(
        functools.partial(tile_kernel, len(right)),
        grid_spec=pltpu.PrefetchScalarGridSpec(
            num_scalar_prefetch=1,
            grid=(both // width,),
            in_specs=specs,
            out_specs=pl.BlockSpec((share, width), lambda n, at: (0, n)),
        ),
        out_shape=jax.ShapeDtypeStruct((share, both), dtype),
        cost_estimate=pl.CostEstimate(
            flops=2 * depth * share * both, bytes_accessed=2 * depth * (share + both), transcendentals=0
        ),
    )(jnp.stack([own, other]), *left, *passed, *right)


def shifted(values, count, stride, extent):
    pairs = []
    for i in range(lax.axis_size("dp")):
        place = i // stride % extent
        pairs.append((i, i + ((place + count) % extent - place) * stride))
    return lax.ppermute(values, "dp", pairs)


def step(tokens, out_grad, weights, master, first_moment, second_moment):
    model_width, _, half_width = weights.shape
    both = 2 * half_width
    flat_weights = weights.reshape(model_width, both)
    local_tokens = tokens.shape[0]
    replicas = lax.axis_size("dp")
    shards = lax.axis_size("tensor")
    shard = lax.axis_index("tensor")
    place = lax.axis_index("dp")
    core, mid, outer = place % 2, place // 2 % 2, place // 4
    outers = replicas // 4
    share = model_width // replicas
    loss_scale = (local_tokens * shards * replicas) ** (-0.5)

    def along_core(values):
        return shifted(values, 1, 1, 2)

    def along_mid(values):
        return shifted(values, 1, 2, 2)

    def along_outer(values):
        return shifted(values, 1, 4, outers)

    def other_columns(block):
        return pick_columns(block, 1 - core, share)

    whole = local_tokens % SEQ == 0
    if whole:
        blocks = [tokens]
        for k in range(1, shards):
            blocks.append(
                lax.ppermute(tokens, "tensor", [(i, (i + k) % shards) for i in range(shards)])
            )
        ups = [
            lax.dynamic_slice_in_dim(out_grad, ((shard - k) % shards) * local_tokens, local_tokens, 0)
            for k in range(shards)
        ]
    else:
        blocks = [lax.all_gather(tokens, "tensor", axis=0, tiled=True)]
        ups = [out_grad]

    def term(k):
        return product(pre_grads[k], flat_weights, (1, 1)).astype(BF16)

    left, passed, swapped, pre_grads = [], [], [], []
    for k, (block, upstream) in enumerate(zip(blocks, ups)):
        left.append(block)
        passed.append(along_core(other_columns(block)))
        projected = jnp.dot(block, flat_weights, preferred_element_type=F32)
        pre_grads.append(local_backward(projected, upstream))
        swapped.append(along_core(pre_grads[k]))

    def partial_of(o, m, dtype):
        tile = o * 2 + m
        return tile_product(tile * 2 + core, tile, left, passed, pre_grads + swapped, share, dtype)

    targets = [(outer - 1 - i) % outers for i in range(outers)]
    crossed = []
    for o in targets:
        away = partial_of(o, 1 - mid, BF16)
        crossed.append(along_mid(away))
    homes = []
    for o in targets:
        homes.append(partial_of(o, mid, F32))
    summed = homes[0] + crossed[0].astype(F32)
    for i in range(1, outers):
        riding = along_outer(summed.astype(BF16))
        summed = homes[i] + crossed[i].astype(F32) + riding.astype(F32)

    gradient = (summed * loss_scale).reshape(share, 2, half_width)
    news = adamw_update(gradient, master, first_moment, second_moment)

    piece = lax.optimization_barrier(news[0].astype(BF16))
    new_weights = jnp.zeros((outers, 2, 2, share, 2, half_width), BF16)
    late = []

    def put(new_weights, piece, o, m, c):
        return lax.dynamic_update_slice(new_weights, piece[None, None, None], (o, m, c, 0, 0, 0))

    for i in range(outers):
        o = (outer - i) % outers
        across = along_mid(piece)
        twin = along_core(piece)
        across_twin = along_core(across)
        new_weights = put(new_weights, piece, o, mid, core)
        new_weights = put(new_weights, twin, o, mid, 1 - core)
        late += [(across, o, 1 - mid, core), (across_twin, o, 1 - mid, 1 - core)]
        while len(late) > 2:
            new_weights = put(new_weights, *late.pop(0))
        if i < outers - 1:
            piece = along_outer(piece)
    for piece_at in late:
        new_weights = put(new_weights, *piece_at)
    new_weights = new_weights.reshape(weights.shape)

    if whole:
        total = term(0).astype(F32)
        for k in range(1, shards):
            sent = term(k)
            got = lax.ppermute(sent, "tensor", [(i, (i - k) % shards) for i in range(shards)])
            total = total + got.astype(F32)
        input_grad = total.astype(BF16)
    else:
        input_grad = lax.psum_scatter(term(0), "tensor", scatter_dimension=0, tiled=True)
    return (input_grad, new_weights, *news)


def solution(mesh):
    state = P("dp", None, "tensor")
    rows = P(("dp", "tensor"), None)
    held = P(None, None, "tensor")
    return jax.shard_map(
        step,
        mesh=mesh,
        in_specs=(rows, P("dp", "tensor"), held, state, state, state),
        out_specs=(rows, held, state, state, state),
        check_vma=False,
    )
```
